32 devices in a mesh: orb: 8 (over z, core), dom: 4 (over y, x).
Axes of the slice: x: 2, y: 2, z: 4, core: 2. Of those that a mesh axis runs over, the one named last changes fastest.
Arguments:
- orbitals: float32 [64, 32, 64, 128], P('orb', 'dom'), may hold values from -6 to 6
- veff: float32 [32, 64, 128], P('dom'), may hold values from -1 to 0
- trials: float32 [8, 32, 64, 128], P('orb', 'dom'), may hold values from -32 to 32
- owners: int32 [2], replicated, may hold values from 0 to 7
- levels: float32 [8], replicated, may hold values from 0.05 to 1
- shift_index: int32 [64], P('orb'), may hold values from 0 to 7
Outputs:
- responses: float32 [8, 32, 64, 128], P('orb', 'dom')
The draws below stay inside these ranges and needn't reach their ends.
Inputs may be any that keep to these rules, and one draw needn't show every extreme that they name: `owners`: an orbital group index. `shift_index`: an index into levels.
All inputs are finite; a program needn't handle non-finite values.
Results may differ from the reference program's by a relative error of at most 0.0001.
Values sent between devices are 32-bit elements; how exact they have to be, the bound alone decides.
No kernel may reach another device: no remote copies, remote signals or barrier semaphores. Data moves between devices by JAX's collectives and lax.ppermute only.
A program may use at most 128 MiB of HBM per device.

```python
import math
import jax
import jax.numpy as jnp
from jax import lax

NY = 64
NZ = 128
APPS = 2
SWEEPS = 4
LEVELS = 8
NX = 32
NORB = 64
SLOTS = 8


def draw_trials(key, part):
    first = jax.random.fold_in(jax.random.fold_in(key, 17), 0)
    position = jnp.arange(NX, dtype=jnp.float32) / (NX - 1)
    rising = jnp.exp(0.5 * math.log(3.0) * position)[None, :, None, None]
    return jnp.clip(jax.random.normal(first, (SLOTS, NX, NY, NZ), jnp.float32) * rising, -32.0, 32.0)


def place_ends(result, own_key, low, largest):
    place = [jax.random.randint(jax.random.fold_in(own_key, axis), (), 0, length) for axis, length in enumerate(result.shape)]
    widest = result.shape.index(max(result.shape))
    neighbour = place[:widest] + [(place[widest] + 1) % result.shape[widest]] + place[widest + 1:]
    return result.at[tuple(place)].set(low).at[tuple(neighbour)].set(largest)


def block_levels(stream_key, shape, cuts, least, top_value):
    factor_of, own = 1.0, jax.random.fold_in(stream_key, 6)
    for dim, shards_of in cuts:
        draws = jnp.exp(jax.random.uniform(jax.random.fold_in(own, dim), (shards_of,), jnp.float32, least / len(cuts), top_value / len(cuts)))
        factor_of = factor_of * jnp.repeat(draws, shape[dim] // shards_of).reshape([-1 if axis == dim else 1 for axis in range(len(shape))])
    return factor_of


def scatter_about(key, dims, spread, reach, cuts=(), kind=jnp.bfloat16):
    array = spread * jax.random.normal(key, dims, jnp.float32)
    if cuts:
        array = array * block_levels(key, dims, cuts, -0.22, 0.18)
    return jnp.clip(array, -reach, reach).astype(kind)


def setup_inputs(seed: int = 0) -> dict:
    key_of = jax.random.split(jax.random.key(seed), 7)
    return {
        "orbitals": scatter_about(key_of[0], (NORB, NX, NY, NZ), 1.0, 6.0, ((0, 8), (1, 4)), jnp.float32),
        "veff": jnp.clip(-1.0 + 1.0 * jax.random.uniform(key_of[1], (NX, NY, NZ), jnp.float32) ** block_levels(key_of[1], (NX, NY, NZ), ((0, 4),), -0.2, 0.2), -1.0, 0.0),
        "trials": draw_trials(jax.random.fold_in(key_of[6], 71), 0),
        "owners": jax.random.randint(key_of[3], (APPS,), 0, SLOTS).astype(jnp.int32),
        "levels": jnp.clip(jnp.exp(jax.random.uniform(key_of[4], (LEVELS,), jnp.float32, math.log(0.05), math.log(1.0))), 0.05, 1.0),
        "shift_index": place_ends(jax.random.randint(key_of[5], (NORB,), 0, LEVELS), jax.random.fold_in(key_of[5], 1), 0, LEVELS - 1).astype(jnp.int32),
    }


stencil_taps = (-49.0 / 18.0, 1.5, -0.15, 1.0 / 90.0)
center_shift = 4.05
center_depth = 5.05
inverse_half = 1.0 / 5.05
norm_epsilon = 1e-06

def apply_map(extended, potential_in):
    inner_count = extended.shape[1] - 6
    width_y = extended.shape[2]
    width_z = extended.shape[3]
    padded = jnp.pad(extended, ((0, 0), (0, 0), (3, 3), (3, 3)))
    middle = padded[:, 3:3 + inner_count, 3:3 + width_y, 3:3 + width_z]
    laplace = 3.0 * stencil_taps[0] * middle
    for offset in (1, 2, 3):
        weight = stencil_taps[offset]
        laplace = laplace + weight * (padded[:, 3 + offset:3 + offset + inner_count, 3:3 + width_y, 3:3 + width_z] + padded[:, 3 - offset:3 - offset + inner_count, 3:3 + width_y, 3:3 + width_z])
        laplace = laplace + weight * (padded[:, 3:3 + inner_count, 3 + offset:3 + offset + width_y, 3:3 + width_z] + padded[:, 3:3 + inner_count, 3 - offset:3 - offset + width_y, 3:3 + width_z])
        laplace = laplace + weight * (padded[:, 3:3 + inner_count, 3:3 + width_y, 3 + offset:3 + offset + width_z] + padded[:, 3:3 + inner_count, 3:3 + width_y, 3 - offset:3 - offset + width_z])
    energy = -0.5 * laplace + potential_in[None] * middle
    return (energy - center_shift * middle) * inverse_half

def coefficients(level_gap):
    ratio_q = (center_depth + level_gap) * inverse_half
    root_term = jnp.sqrt(ratio_q * ratio_q - 1.0)
    decay = ratio_q - root_term
    first = -inverse_half / root_term
    series = [first]
    current = first * (-2.0 * decay)
    series.append(current)
    for offset in range(2, SWEEPS + 1):
        current = current * -decay
        series.append(current)
    return series

def global_map(field, veff):
    extended = jnp.pad(field[None], ((0, 0), (3, 3), (0, 0), (0, 0)))
    return apply_map(extended, veff)[0]

def filtered(initial, veff, series):
    summed = series[0] * initial
    previous = initial
    current = global_map(initial, veff)
    summed = summed + series[1] * current
    for offset in range(2, SWEEPS + 1):
        following = 2.0 * global_map(current, veff) - previous
        summed = summed + series[offset] * following
        previous = current
        current = following
    return summed

def reference(orbitals, veff, trials, owners, levels, shift_index):
    grid_cells = NX * NY * NZ
    level_gaps = levels[shift_index]
    responses = jnp.zeros((SLOTS, NX, NY, NZ), jnp.float32)
    slot_ids = jnp.arange(SLOTS, dtype=jnp.int32)
    for app_index in range(APPS):
        chosen_trial = lax.dynamic_index_in_dim(trials, owners[app_index], 0, keepdims=False)
        potential = chosen_trial * lax.rsqrt(jnp.sum(chosen_trial * chosen_trial) / grid_cells + norm_epsilon)

        def add_orbital(running, inputs):
            orbital, level_gap = inputs
            series = coefficients(level_gap)
            delta = filtered(potential * orbital, veff, series)
            return (running + orbital * delta, None)
        running, unused = lax.scan(add_orbital, jnp.zeros((NX, NY, NZ), jnp.float32), (orbitals, level_gaps))
        response = running * (4.0 / NORB)
        chosen = (slot_ids == owners[app_index])[:, None, None, None]
        responses = responses + jnp.where(chosen, response[None], 0.0)
    return responses
```

```python
import functools

import jax
import jax.numpy as jnp
import numpy as np
from jax import lax
from jax.experimental import pallas as pl
from jax.experimental.pallas import tpu as pltpu
from jax.sharding import PartitionSpec as P


SWEEPS = 4
SUB = 8
PLANES = 16
center_depth = 5.05
inverse_half = 1.0 / 5.05
norm_epsilon = 1e-06
step = -1.0 / (180.0 * 5.05)
taps = (135.0, -13.5, 1.0)


def monomials(level_gap):
    ratio_q = (center_depth + level_gap) * inverse_half
    root_term = jnp.sqrt(ratio_q * ratio_q - 1.0)
    decay = ratio_q - root_term
    c0 = -inverse_half / root_term
    c1 = c0 * (-2.0 * decay)
    c2 = c1 * -decay
    c3 = c2 * -decay
    c4 = c3 * -decay
    m = (c0 - c2 + c4, c1 - 3.0 * c3, 2.0 * c2 - 8.0 * c4, 4.0 * c3, 8.0 * c4)
    rows = [m[k] / m[4] * np.float32(step ** (k - SWEEPS)) for k in range(SWEEPS)]
    return jnp.stack(rows + [m[4] * np.float32(step**SWEEPS)], axis=-1)


def lane_matrix(width):
    index = np.arange(width)
    apart = np.abs(index[:, None] - index[None, :])
    matrix = sum(np.where(apart == j + 1, taps[j], 0.0) for j in range(3))
    return jnp.asarray(np.concatenate([matrix, matrix], axis=0), jnp.bfloat16)


def folded(array):
    shape = array.shape
    return array.reshape(shape[:-2] + (SUB, shape[-2] // SUB, shape[-1])).swapaxes(-3, -2)


def put(target, plane, value):
    depth = value.shape[0]
    target[plane + 3, 3 : 3 + depth] = value
    row = lax.broadcasted_iota(jnp.int32, (3,) + value.shape[1:], 1)
    target[plane + 3, 0:3] = jnp.where(row == 0, 0.0, pltpu.roll(value[depth - 3 :], 1, 1))
    target[plane + 3, 3 + depth :] = jnp.where(row == SUB - 1, 0.0, pltpu.roll(value[:3], SUB - 1, 1))


def stage(source, start, centre, matrix, weight, planes, depth, finish):
    def body(block, carry):
        first = block * planes
        middle = source[pl.ds(first + 3, planes), 3 : 3 + depth]
        flat = middle.reshape(planes * depth * SUB, middle.shape[-1])
        high = flat.astype(jnp.bfloat16)
        low = (flat - high.astype(jnp.float32)).astype(jnp.bfloat16)
        along = jnp.dot(
            jnp.concatenate([high, low], axis=1), matrix[...], preferred_element_type=jnp.float32
        ).reshape(middle.shape)
        for p in range(planes):
            x = first + p
            row = source[x + 3]

            def pair(j):
                across = source[x + 3 - j, 3 : 3 + depth] + source[x + 3 + j, 3 : 3 + depth]
                return across + (row[3 - j : 3 - j + depth] + row[3 + j : 3 + j + depth])

            total = along[p] + pair(3)
            total = total + taps[1] * pair(2)
            total = total + taps[0] * pair(1)
            total = total + centre[x] * row[3 : 3 + depth]
            total = total + weight * start[x + 3, 3 : 3 + depth]
            finish(x, total)
        return carry

    lax.fori_loop(0, (source.shape[0] - 6) // planes, body, 0)


def chunk_kernel(groups, slab, depth, cells, final_scale, accumulate, *refs):
    place_ref, weight_ref = refs[:2]
    refs = list(refs[2:])
    matrix = refs.pop(0)
    orb_refs = [[refs.pop(0) for _ in range(groups)] for _ in range(2)]
    pot_refs = [refs.pop(0) for _ in range(groups)]
    veff_own = refs.pop(0)
    veff_refs = [[refs.pop(0) for _ in range(groups - 1)] for _ in range(2)]
    before = refs.pop(0) if accumulate else None
    out, first, second, third, pot, centre, orb = refs
    total = groups * slab
    my_dom, my_rest, my_core = place_ref[0], place_ref[1], place_ref[2]
    pieces = pot_refs[0].shape[0]
    piece = pot_refs[0].shape[1]
    half = slab // 2
    blank = jnp.zeros((3,) + first.shape[1:], jnp.float32)
    for buffer in (first, second, third):
        buffer[0:3] = blank
        buffer[total + 3 :] = blank

    squares = jnp.zeros((depth, SUB, first.shape[-1]), jnp.float32)
    for k in range(groups):
        base = (my_dom ^ k) * slab

        def load_pot(i, carry, k=k, base=base):
            for j in range(pieces):
                value = pot_refs[k][j, i]
                pot[base + (my_rest ^ j) * piece + i] = value
                carry = carry + value * value
            return carry

        squares = lax.fori_loop(0, piece, load_pot, squares)

        def load_veff(i, carry, k=k, base=base):
            if k == 0:
                centre[base + i] = -180.0 * veff_own[i] - 6.0
            else:
                centre[base + my_core * half + i] = -180.0 * veff_refs[0][k - 1][i] - 6.0
                centre[base + (1 - my_core) * half + i] = -180.0 * veff_refs[1][k - 1][i] - 6.0
            return carry

        lax.fori_loop(0, slab if k == 0 else half, load_veff, 0)
    mean = jnp.sum(jnp.sum(jnp.sum(squares, axis=0), axis=0, keepdims=True), axis=1, keepdims=True) / cells
    scale = lax.rsqrt(mean + norm_epsilon) * final_scale

    for n in range(2):
        for k in range(groups):
            base = (my_dom ^ k) * slab

            def load_orb(i, carry, k=k, base=base, n=n):
                value = orb_refs[n][k][i]
                orb[base + i] = value
                put(first, base + i, value * pot[base + i])
                return carry

            lax.fori_loop(0, slab, load_orb, 0)

        planes = PLANES
        run = functools.partial(stage, start=first, centre=centre, matrix=matrix, planes=planes, depth=depth)
        run(first, weight=weight_ref[n, 3], finish=lambda x, value: put(second, x, value))
        run(second, weight=weight_ref[n, 2], finish=lambda x, value: put(third, x, value))
        run(third, weight=weight_ref[n, 1], finish=lambda x, value: put(second, x, value))

        def finish(x, value, n=n):
            value = value * orb[x] * (scale * weight_ref[n, 4])
            if n == 0:
                out[x] = value + before[x] if accumulate else value
            else:
                out[x] = out[x] + value

        run(second, weight=weight_ref[n, 0], finish=finish)


def run_chunk(place, weights, matrix, orbs, pots, veff_own, veffs, before, cells, final_scale):
    groups = len(pots)
    slab = orbs[0][0].shape[0]
    depth, sub, width = orbs[0][0].shape[1:]
    total = groups * slab
    operands = [place, weights, matrix] + orbs[0] + orbs[1] + pots + [veff_own] + veffs[0] + veffs[1]
    if before is not None:
        operands.append(before)
    padded = pltpu.VMEM((total + 6, depth + 6, sub, width), jnp.float32)
    plain = pltpu.VMEM((total, depth, sub, width), jnp.float32)
    body = functools.partial(chunk_kernel, groups, slab, depth, cells, final_scale, before is not None)
    vmem, smem = pl.BlockSpec(memory_space=pltpu.VMEM), pl.BlockSpec(memory_space=pltpu.SMEM)
    return pl.pallas_call(
        body,
        out_shape=jax.ShapeDtypeStruct((total, depth, sub, width), jnp.float32),
        in_specs=[smem, smem] + [vmem] * (len(operands) - 2),
        out_specs=vmem,
        scratch_shapes=[padded] * 3 + [plain] * 3,
        cost_estimate=pl.CostEstimate(flops=200 * total * depth * sub * width, bytes_accessed=4 * total * depth * sub * width, transcendentals=0),
        name="chunk",
    )(*operands)


def per_device(orbitals, veff, trials, owners, levels, shift_index):
    groups, ranks = lax.axis_size("dom"), lax.axis_size("orb")
    rest = ranks // 2
    my_dom, my_rank = lax.axis_index("dom"), lax.axis_index("orb")
    my_rest, my_core = my_rank // 2, my_rank % 2
    local, slab = orbitals.shape[:2]
    cells = slab * groups * orbitals.shape[2] * orbitals.shape[3]
    chunks = local // groups
    final_scale = 4.0 / (local * ranks)

    def over_dom(array, k):
        return lax.ppermute(array, "dom", [(i, i ^ k) for i in range(groups)])

    def over_rest(array, k):
        return lax.ppermute(array, "orb", [(i, i ^ (2 * k)) for i in range(ranks)])

    def over_core(array):
        return lax.ppermute(array, "orb", [(i, i ^ 1) for i in range(ranks)])

    def at(array, index):
        return lax.dynamic_index_in_dim(array, index, 0, keepdims=False)

    orbitals = folded(orbitals)
    veff = folded(veff)
    trial = folded(trials[0])

    swapped_trial = over_core(trial)
    owner = owners[my_core]
    held = jnp.where(owner % 2 == my_core, trial, swapped_trial)
    held = held.reshape((rest, slab // rest) + held.shape[1:])
    from_rest = [at(held, my_rest)] + [over_rest(at(held, my_rest ^ k), k) for k in range(1, rest)]
    which = (owner // 2) ^ my_rest
    mine = from_rest[0]
    for k in range(1, rest):
        mine = jnp.where(which == k, from_rest[k], mine)
    spread = jnp.stack([mine] + [over_rest(mine, k) for k in range(1, rest)])
    pots = [spread] + [over_dom(spread, k) for k in range(1, groups)]

    half = slab // 2
    own_half = lax.dynamic_slice_in_dim(veff, my_core * half, half, 0)
    veff_mine = [over_dom(own_half, k) for k in range(1, groups)]
    veff_other = [over_core(array) for array in veff_mine]

    chosen = shift_index[:, None] == jnp.arange(levels.shape[0], dtype=jnp.int32)[None, :]
    weights = monomials(jnp.sum(jnp.where(chosen, levels[None, :], 0.0), axis=1))
    other_weights = over_core(weights)
    place = jnp.stack([my_dom, my_rest, my_core]).astype(jnp.int32)
    matrix = lane_matrix(orbitals.shape[-1])

    response = None
    for chunk in range(chunks):
        parts = [at(orbitals, my_dom * chunks + chunk)]
        parts += [over_dom(at(orbitals, (my_dom ^ k) * chunks + chunk), k) for k in range(1, groups)]
        others = [over_core(part) for part in parts]
        pair = jnp.stack([at(weights, my_dom * chunks + chunk), at(other_weights, my_dom * chunks + chunk)])
        response = run_chunk(
            place, pair, matrix, [parts, others], pots, veff, [veff_mine, veff_other], response, cells, final_scale
        )

    slabs = response.reshape((groups, slab) + response.shape[1:])
    summed = at(slabs, my_dom)
    for k in range(1, groups):
        summed = summed + over_dom(at(slabs, my_dom ^ k), k)
    pieces = summed.reshape((rest, slab // rest) + summed.shape[1:])
    piece = at(pieces, my_rest)
    for k in range(1, rest):
        piece = piece + over_rest(at(pieces, my_rest ^ k), k)
    gathered = [piece] + [over_rest(piece, k) for k in range(1, rest)]
    order = [gathered[0]] * rest
    full = jnp.zeros_like(summed)
    for k in range(rest):
        full = lax.dynamic_update_slice_in_dim(full, gathered[k], (my_rest ^ k) * (slab // rest), 0)
    swapped = over_core(full)
    result = jnp.where(owner == my_rank, full, 0.0) + jnp.where(owners[1 - my_core] == my_rank, swapped, 0.0)
    result = result.swapaxes(-3, -2)
    return result.reshape((1, slab) + (result.shape[1] * result.shape[2], result.shape[3]))


def solution(mesh):
    placed = (
        P("orb", "dom", None, None),
        P("dom", None, None),
        P("orb", "dom", None, None),
        P(),
        P(),
        P("orb"),
    )
    return jax.shard_map(
        per_device,
        mesh=mesh,
        in_specs=placed,
        out_specs=P("orb", "dom", None, None),
        check_vma=False,
    )
```

```python
import functools

import jax
import jax.numpy as jnp
import numpy as np
from jax import lax
from jax.experimental import pallas as pl
from jax.experimental.pallas import tpu as pltpu
from jax.sharding import PartitionSpec as P


SWEEPS = 4
SUB = 8
PLANES = 16
center_depth = 5.05
inverse_half = 1.0 / 5.05
norm_epsilon = 1e-06
step = -1.0 / (180.0 * 5.05)
taps = (135.0, -13.5, 1.0)

VMEM = pl.BlockSpec(memory_space=pltpu.VMEM)
SMEM = pl.BlockSpec(memory_space=pltpu.SMEM)
ANY = pl.BlockSpec(memory_space=pl.ANY)


def monomial_kernel(level_ref, index_ref, out):
    for n in range(out.shape[0]):
        level_gap = jnp.full(out.shape[2:], level_ref[index_ref[n]], jnp.float32)
        ratio_q = (center_depth + level_gap) * inverse_half
        root_term = jnp.sqrt(ratio_q * ratio_q - 1.0)
        decay = ratio_q - root_term
        c0 = -inverse_half / root_term
        c1 = c0 * (-2.0 * decay)
        c2 = c1 * -decay
        c3 = c2 * -decay
        c4 = c3 * -decay
        m = (c0 - c2 + c4, c1 - 3.0 * c3, 2.0 * c2 - 8.0 * c4, 4.0 * c3, 8.0 * c4)
        for k in range(SWEEPS):
            out[n, k] = m[k] / m[4] * np.float32(step ** (k - SWEEPS))
        out[n, SWEEPS] = m[4] * np.float32(step**SWEEPS)


def monomials(levels, shift_index, width):
    shape = (shift_index.shape[0], SWEEPS + 1, SUB, width)
    return pl.pallas_call(
        monomial_kernel,
        out_shape=jax.ShapeDtypeStruct(shape, jnp.float32),
        in_specs=[SMEM, SMEM],
        out_specs=VMEM,
        compiler_params=pltpu.CompilerParams(vmem_limit_bytes=2 << 20),
        name="monomials",
    )(levels, shift_index)


def lane_matrix(width):
    index = np.arange(width)
    apart = np.abs(index[:, None] - index[None, :])
    matrix = sum(np.where(apart == j + 1, taps[j], 0.0) for j in range(3))
    return jnp.asarray(np.concatenate([matrix, matrix], axis=0), jnp.bfloat16)


def folded(ref, *index):
    depth = ref.shape[-2] // SUB
    return jnp.stack([ref[(*index, pl.ds(y, SUB, stride=depth), slice(None))] for y in range(depth)])


def put(target, plane, value):
    depth = value.shape[0]
    target[plane + 3, 3 : 3 + depth] = value
    row = lax.broadcasted_iota(jnp.int32, (3,) + value.shape[1:], 1)
    target[plane + 3, 0:3] = jnp.where(row == 0, 0.0, pltpu.roll(value[depth - 3 :], 1, 1))
    target[plane + 3, 3 + depth :] = jnp.where(row == SUB - 1, 0.0, pltpu.roll(value[:3], SUB - 1, 1))


def stage(source, start, centre, matrix, weight, planes, depth, finish):
    def body(block, carry):
        first = block * planes
        middle = source[pl.ds(first + 3, planes), 3 : 3 + depth]
        flat = middle.reshape(planes * depth * SUB, middle.shape[-1])
        high = flat.astype(jnp.bfloat16)
        low = (flat - high.astype(jnp.float32)).astype(jnp.bfloat16)
        along = jnp.dot(
            jnp.concatenate([high, low], axis=1), matrix[...], preferred_element_type=jnp.float32
        ).reshape(middle.shape)
        for p in range(planes):
            x = first + p
            row = source[x + 3]

            def pair(j):
                across = source[x + 3 - j, 3 : 3 + depth] + source[x + 3 + j, 3 : 3 + depth]
                return across + (row[3 - j : 3 - j + depth] + row[3 + j : 3 + j + depth])

            total = along[p] + pair(3)
            total = total + taps[1] * pair(2)
            total = total + taps[0] * pair(1)
            total = total + centre[x] * row[3 : 3 + depth]
            total = total + weight * start[x + 3, 3 : 3 + depth]
            finish(x, total)
        return carry

    lax.fori_loop(0, (source.shape[0] - 6) // planes, body, 0)


def stash_kernel(groups, slab, vectors, *refs):
    refs = list(refs)
    place_ref = refs.pop(0)
    orb_refs = [[refs.pop(0) for _ in range(groups)] for _ in range(vectors)]
    veff_own = refs.pop(0)
    veff_refs = [[refs.pop(0) for _ in range(groups - 1)] for _ in range(2)]
    orb, centre = refs
    my_dom, my_core = place_ref[0], place_ref[2]
    half = slab // 2
    for k in range(groups):
        base = (my_dom ^ k) * slab

        def load_orb(i, carry, k=k, base=base):
            for n in range(vectors):
                orb[n, base + i] = folded(orb_refs[n][k], i)
            return carry

        lax.fori_loop(0, slab, load_orb, 0)

        def load_veff(i, carry, k=k, base=base):
            if k == 0:
                centre[base + i] = -180.0 * folded(veff_own, i) - 6.0
            else:
                centre[base + my_core * half + i] = -180.0 * folded(veff_refs[0][k - 1], i) - 6.0
                centre[base + (1 - my_core) * half + i] = -180.0 * folded(veff_refs[1][k - 1], i) - 6.0
            return carry

        lax.fori_loop(0, slab if k == 0 else half, load_veff, 0)


def stash(place, orbs, veff_own, veffs):
    groups, vectors = len(orbs[0]), len(orbs)
    slab, rows, width = orbs[0][0].shape
    grid = (groups * slab, rows // SUB, SUB, width)
    operands = [place] + [piece for pieces in orbs for piece in pieces] + [veff_own] + veffs[0] + veffs[1]
    size = grid[0] * rows * width
    return pl.pallas_call(
        functools.partial(stash_kernel, groups, slab, vectors),
        out_shape=[jax.ShapeDtypeStruct(shape, jnp.float32) for shape in ((vectors,) + grid, grid)],
        in_specs=[SMEM] + [VMEM] * (len(operands) - 1),
        out_specs=[VMEM, VMEM],
        cost_estimate=pl.CostEstimate(flops=4 * size, bytes_accessed=8 * size * (vectors + 1), transcendentals=0),
        compiler_params=pltpu.CompilerParams(vmem_limit_bytes=8 * size * (vectors + 1) + (3 << 20)),
        name="stash",
    )(*operands)


def sweep_kernel(layout, *refs):
    groups, slab, cells, final_scale, vectors, prepared, accumulate, chunk, chunks = layout
    refs = list(refs)
    place_ref = refs.pop(0)
    weight_refs = [refs.pop(0) for _ in range(vectors)]
    matrix, centre = refs.pop(0), refs.pop(0)
    if prepared:
        orb_refs = [refs.pop(0) for _ in range(groups)]
        pot, scale_ref = refs.pop(0), refs.pop(0)
    else:
        orb_all = refs.pop(0)
        pot_refs = [refs.pop(0) for _ in range(groups)]
    before = refs.pop(0) if accumulate else None
    out = refs.pop(0)
    if not prepared:
        pot, scale_ref = refs.pop(0), refs.pop(0)
    first, second, third = refs[:3]
    total = groups * slab
    depth = first.shape[1] - 6
    my_dom, my_rest = place_ref[0], place_ref[1]

    copies = []
    if prepared:
        orb, orb_raw, orb_sem = refs[3:]
        for k in range(groups):
            target = orb_raw.at[pl.ds((my_dom ^ k) * slab, slab)]
            copies.append(pltpu.make_async_copy(orb_refs[k], target, orb_sem.at[k]))
            copies[-1].start()

    blank = jnp.zeros((3,) + first.shape[1:], jnp.float32)
    for buffer in (first, second, third):
        buffer[0:3] = blank
        buffer[total + 3 :] = blank

    if not prepared:
        pieces, piece = pot_refs[0].shape[:2]
        squares = jnp.zeros(pot.shape[1:], jnp.float32)
        for k in range(groups):
            base = (my_dom ^ k) * slab

            def load_pot(i, carry, k=k, base=base):
                for j in range(pieces):
                    value = folded(pot_refs[k], j, i)
                    x = base + (my_rest ^ j) * piece + i
                    pot[x] = value
                    put(first, x, value * orb_all[0, x])
                    carry = carry + value * value
                return carry

            squares = lax.fori_loop(0, piece, load_pot, squares)
        mean = jnp.sum(jnp.sum(jnp.sum(squares, axis=0), axis=0, keepdims=True), axis=1, keepdims=True) / cells
        scale_ref[...] = jnp.broadcast_to(lax.rsqrt(mean + norm_epsilon) * final_scale, scale_ref.shape)
    scale = scale_ref[...]
    orbital = my_dom * chunks + chunk
    for copy in copies:
        copy.wait()

    for n in range(vectors):
        weight_ref = weight_refs[n]
        if prepared or n:

            def load_orb(x, carry, n=n):
                value = folded(orb_raw, x) if prepared else orb_all[n, x]
                if prepared:
                    orb[x] = value
                put(first, x, value * pot[x])
                return carry

            lax.fori_loop(0, total, load_orb, 0)

        run = functools.partial(stage, start=first, centre=centre, matrix=matrix, planes=PLANES, depth=depth)
        run(first, weight=weight_ref[orbital, 3], finish=lambda x, value: put(second, x, value))
        run(second, weight=weight_ref[orbital, 2], finish=lambda x, value: put(third, x, value))
        run(third, weight=weight_ref[orbital, 1], finish=lambda x, value: put(second, x, value))
        factor = scale * weight_ref[orbital, SWEEPS]

        def finish(x, value, n=n, factor=factor):
            value = value * (orb[x] if prepared else orb_all[n, x]) * factor
            if n == 0:
                out[x] = value + before[x] if accumulate else value
            else:
                out[x] = out[x] + value

        run(second, weight=weight_ref[orbital, 0], finish=finish)


def sweep(place, weights, matrix, centre, orbs, fields, before, cells, final_scale, chunk, chunks):
    prepared = isinstance(orbs, list)
    vectors = len(weights)
    total, depth, sub, width = grid = centre.shape
    rows = depth * sub
    groups = len(orbs) if prepared else len(fields)
    size = total * rows * width
    flat = list(orbs) if prepared else [orbs]
    operands = [place, *weights, matrix, centre] + flat + fields
    specs = [SMEM] + [VMEM] * (vectors + 2) + [ANY if prepared else VMEM] * len(flat) + [VMEM] * len(fields)
    if before is not None:
        operands.append(before)
        specs.append(VMEM)
    shapes = [grid] if prepared else [grid, grid, (sub, width)]
    scratch = [pltpu.VMEM((total + 6, depth + 6, sub, width), jnp.float32)] * 3
    if prepared:
        scratch += [pltpu.VMEM(grid, jnp.float32), pltpu.VMEM((total, rows, width), jnp.float32)]
        scratch.append(pltpu.SemaphoreType.DMA((groups,)))
    used = 12 * (total + 6) * (depth + 6) * sub * width + 4 * size * (6 if prepared else 4 + vectors)
    layout = (groups, total // groups, cells, final_scale, vectors, prepared, before is not None, chunk, chunks)
    return pl.pallas_call(
        functools.partial(sweep_kernel, layout),
        out_shape=[jax.ShapeDtypeStruct(shape, jnp.float32) for shape in shapes],
        in_specs=specs,
        out_specs=[VMEM] * len(shapes),
        scratch_shapes=scratch,
        cost_estimate=pl.CostEstimate(flops=200 * size * vectors, bytes_accessed=16 * size, transcendentals=0),
        compiler_params=pltpu.CompilerParams(vmem_limit_bytes=used + (3 << 20)),
    )(*operands)


def pick_kernel(rest, place_ref, owner_ref, *refs):
    out = refs[-1]
    my_rest, my_core = place_ref[1], place_ref[2]
    owner = owner_ref[my_core]
    wanted = 2 * ((owner >> 1) ^ my_rest) + ((owner & 1) ^ my_core)
    for index in range(2 * rest):

        @pl.when(wanted == index)
        def take(index=index):
            out[...] = refs[index][...]


def pick(place, owners, pieces):
    return pl.pallas_call(
        functools.partial(pick_kernel, len(pieces) // 2),
        out_shape=jax.ShapeDtypeStruct(pieces[0].shape, jnp.float32),
        in_specs=[SMEM, SMEM] + [VMEM] * len(pieces),
        out_specs=VMEM,
        compiler_params=pltpu.CompilerParams(vmem_limit_bytes=(2 << 20) + 4 * pieces[0].size * (len(pieces) + 1)),
        name="pick",
    )(place, owners, *pieces)


def join_kernel(*refs):
    for k, ref in enumerate(refs[:-1]):
        refs[-1][k] = ref[...]


def join(pieces):
    return pl.pallas_call(
        join_kernel,
        out_shape=jax.ShapeDtypeStruct((len(pieces),) + pieces[0].shape, jnp.float32),
        in_specs=[VMEM] * len(pieces),
        out_specs=VMEM,
        compiler_params=pltpu.CompilerParams(vmem_limit_bytes=(2 << 20) + 8 * len(pieces) * pieces[0].size),
        name="join",
    )(*pieces)


def deliver_kernel(rest, place_ref, owner_ref, *refs):
    out = refs[-1]
    my_rest, my_core, my_rank = place_ref[1], place_ref[2], place_ref[3]
    keep = (owner_ref[my_core] == my_rank).astype(jnp.float32)
    take = (owner_ref[1 - my_core] == my_rank).astype(jnp.float32)
    piece, depth = refs[0].shape[:2]
    for k in range(rest):
        for i in range(piece):
            value = refs[2 * k][i] * keep + refs[2 * k + 1][i] * take
            for y in range(depth):
                out[0, (my_rest ^ k) * piece + i, pl.ds(y, SUB, stride=depth), :] = value[y]


def deliver(place, owners, pieces):
    rest = len(pieces) // 2
    piece, depth, sub, width = pieces[0].shape
    return pl.pallas_call(
        functools.partial(deliver_kernel, rest),
        out_shape=jax.ShapeDtypeStruct((1, rest * piece, depth * sub, width), jnp.float32),
        in_specs=[SMEM, SMEM] + [VMEM] * len(pieces),
        out_specs=VMEM,
        compiler_params=pltpu.CompilerParams(vmem_limit_bytes=(2 << 20) + 4 * pieces[0].size * 3 * rest),
        name="deliver",
    )(place, owners, *pieces)


def per_device(orbitals, veff, trials, owners, levels, shift_index):
    groups, ranks = lax.axis_size("dom"), lax.axis_size("orb")
    rest = ranks // 2
    my_dom, my_rank = lax.axis_index("dom"), lax.axis_index("orb")
    my_rest, my_core = my_rank // 2, my_rank % 2
    local, slab = orbitals.shape[:2]
    cells = slab * groups * orbitals.shape[2] * orbitals.shape[3]
    chunks = local // groups
    final_scale = 4.0 / (local * ranks)

    def send(array, axis, size, flip):
        return lax.ppermute(array, axis, [(i, i ^ flip) for i in range(size)])

    def over_dom(pick):
        return {k: send(pick(k), "dom", groups, k) for k in reversed(range(1, groups))}

    def over_rest(pick):
        return {k: send(pick(k), "orb", ranks, 2 * k) for k in reversed(range(1, rest))}

    def over_core(array):
        return send(array, "orb", ranks, 1)

    def at(array, index):
        return lax.dynamic_index_in_dim(array, index, 0, keepdims=False)

    def chunk_of(chunk):
        parts = over_dom(lambda k: at(orbitals, (my_dom ^ k) * chunks + chunk))
        parts[0] = at(orbitals, my_dom * chunks + chunk)
        return [parts[k] for k in range(groups)]

    half, piece = slab // 2, slab // rest

    held = trials[0].reshape((rest, piece) + trials.shape[2:])
    arrived = over_rest(lambda k: at(held, my_rest ^ k))
    arrived[0] = at(held, my_rest)
    parts = [chunk_of(0)]
    crossed = {k: over_core(arrived[k]) for k in (0, *reversed(range(1, rest)))}
    place = jnp.stack([my_dom, my_rest, my_core, my_rank]).astype(jnp.int32)
    mine = pick(place, owners, [array[k] for k in range(rest) for array in (arrived, crossed)])
    spread = over_rest(lambda k: mine)
    own_half = lax.dynamic_slice_in_dim(veff, my_core * half, half, 0)
    veff_mine = over_dom(lambda k: own_half)
    spread = join([mine] + [spread[k] for k in range(1, rest)])
    pots = over_dom(lambda k: spread)
    pots[0] = spread
    pots = [pots[k] for k in range(groups)]

    weights = monomials(levels, shift_index, orbitals.shape[-1])
    other_weights = over_core(weights)
    veff_mine = [veff_mine[k] for k in range(1, groups)]
    others = [[over_core(part) for part in parts[0]]]
    veff_other = [over_core(array) for array in veff_mine]
    parts += [chunk_of(chunk) for chunk in range(1, chunks)]

    matrix = lane_matrix(orbitals.shape[-1])
    orbs, centre = stash(place, [parts[0], others[0]], veff, [veff_mine, veff_other])
    response, *prepared = sweep(
        place, [weights, other_weights], matrix, centre, orbs, pots, None, cells, final_scale, 0, chunks
    )
    for chunk in range(1, chunks):
        others.append([over_core(part) for part in parts[chunk]])
        for weight, pieces in ((weights, parts), (other_weights, others)):
            response = sweep(
                place, [weight], matrix, centre, pieces[chunk], prepared, response, cells, final_scale, chunk, chunks
            )[0]

    slabs = response.reshape((groups, slab) + response.shape[1:])
    arrived = over_dom(lambda k: at(slabs, my_dom ^ k))
    summed = at(slabs, my_dom)
    for k in range(1, groups):
        summed = summed + arrived[k]
    pieces = summed.reshape((rest, piece) + summed.shape[1:])
    arrived = over_rest(lambda k: at(pieces, my_rest ^ k))
    total = at(pieces, my_rest)
    for k in range(1, rest):
        total = total + arrived[k]
    gathered = over_rest(lambda k: total)
    gathered[0] = total
    crossed = {k: over_core(gathered[k]) for k in (0, *reversed(range(1, rest)))}
    return deliver(place, owners, [array[k] for k in range(rest) for array in (gathered, crossed)])


def solution(mesh):
    placed = (
        P("orb", "dom", None, None),
        P("dom", None, None),
        P("orb", "dom", None, None),
        P(),
        P(),
        P("orb"),
    )
    return jax.shard_map(
        per_device,
        mesh=mesh,
        in_specs=placed,
        out_specs=P("orb", "dom", None, None),
        check_vma=False,
    )
```

```python
import functools

import jax
import jax.numpy as jnp
import numpy as np
from jax import lax
from jax.experimental import pallas as pl
from jax.experimental.pallas import tpu as pltpu
from jax.sharding import PartitionSpec as P


SWEEPS = 4
SUB = 8
PLANES = 32
PHASES = 2
center_depth = 5.05
inverse_half = 1.0 / 5.05
norm_epsilon = 1e-06
step = -1.0 / (180.0 * 5.05)
taps = (135.0, -13.5, 1.0)

VMEM = pl.BlockSpec(memory_space=pltpu.VMEM)
SMEM = pl.BlockSpec(memory_space=pltpu.SMEM)


def monomial_kernel(level_ref, index_ref, out):
    for n in range(out.shape[0]):
        level_gap = jnp.full(out.shape[2:], level_ref[index_ref[n]], jnp.float32)
        ratio_q = (center_depth + level_gap) * inverse_half
        root_term = jnp.sqrt(ratio_q * ratio_q - 1.0)
        decay = ratio_q - root_term
        c0 = -inverse_half / root_term
        c1 = c0 * (-2.0 * decay)
        c2 = c1 * -decay
        c3 = c2 * -decay
        c4 = c3 * -decay
        m = (c0 - c2 + c4, c1 - 3.0 * c3, 2.0 * c2 - 8.0 * c4, 4.0 * c3, 8.0 * c4)
        for k in range(SWEEPS):
            out[n, k] = m[k] / m[4] * np.float32(step ** (k - SWEEPS))
        out[n, SWEEPS] = m[4] * np.float32(step**SWEEPS)


def monomials(levels, shift_index, width):
    shape = (shift_index.shape[0], SWEEPS + 1, SUB, width)
    return pl.pallas_call(
        monomial_kernel,
        out_shape=jax.ShapeDtypeStruct(shape, jnp.float32),
        in_specs=[SMEM, SMEM],
        out_specs=VMEM,
        compiler_params=pltpu.CompilerParams(vmem_limit_bytes=2 << 20),
        name="monomials",
    )(levels, shift_index)


def lane_matrix(width):
    index = np.arange(width)
    apart = np.abs(index[:, None] - index[None, :])
    matrix = sum(np.where(apart == j + 1, taps[j], 0.0) for j in range(3))
    return jnp.asarray(np.concatenate([matrix, matrix], axis=0), jnp.bfloat16)


def folded(ref, *index):
    depth = ref.shape[-2] // SUB
    return jnp.stack([ref[(*index, pl.ds(y, SUB, stride=depth), slice(None))] for y in range(depth)])


def put(target, plane, value):
    depth = value.shape[0]
    target[plane + 3, 3 : 3 + depth] = value
    row = lax.broadcasted_iota(jnp.int32, (3,) + value.shape[1:], 1)
    target[plane + 3, 0:3] = jnp.where(row == 0, 0.0, pltpu.roll(value[depth - 3 :], 1, 1))
    target[plane + 3, 3 + depth :] = jnp.where(row == SUB - 1, 0.0, pltpu.roll(value[:3], SUB - 1, 1))


def stage(source, start, centre, matrix, weight, planes, depth, finish):
    def body(block, carry):
        first = block * planes
        middle = source[pl.ds(first + 3, planes), 3 : 3 + depth]
        flat = middle.reshape(planes * depth * SUB, middle.shape[-1])
        high = flat.astype(jnp.bfloat16)
        low = (flat - high.astype(jnp.float32)).astype(jnp.bfloat16)
        along = jnp.dot(
            jnp.concatenate([high, low], axis=1), matrix[...], preferred_element_type=jnp.float32
        ).reshape(middle.shape)
        for p in range(planes):
            x = first + p
            row = source[x + 3]

            def pair(j):
                across = source[x + 3 - j, 3 : 3 + depth] + source[x + 3 + j, 3 : 3 + depth]
                return across + (row[3 - j : 3 - j + depth] + row[3 + j : 3 + j + depth])

            total = along[p] + pair(3)
            total = total + taps[1] * pair(2)
            total = total + taps[0] * pair(1)
            if start is source:
                total = total + (centre[x] + weight) * row[3 : 3 + depth]
            else:
                total = total + centre[x] * row[3 : 3 + depth]
                total = total + weight * start[x + 3, 3 : 3 + depth]
            finish(x, total)
        return carry

    lax.fori_loop(0, (source.shape[0] - 6) // planes, body, 0)


def stash_kernel(groups, slab, vectors, *refs):
    refs = list(refs)
    place_ref = refs.pop(0)
    orb_refs = [[refs.pop(0) for _ in range(groups)] for _ in range(vectors)]
    veff_own = refs.pop(0)
    veff_refs = [[refs.pop(0) for _ in range(groups - 1)] for _ in range(2)]
    orb, centre = refs
    my_dom, my_core = place_ref[0], place_ref[2]
    half = slab // 2
    for k in range(groups):
        base = (my_dom ^ k) * slab

        def load_orb(i, carry, k=k, base=base):
            for n in range(vectors):
                orb[n, base + i] = folded(orb_refs[n][k], i)
            return carry

        lax.fori_loop(0, slab, load_orb, 0)

        def load_veff(i, carry, k=k, base=base):
            if k == 0:
                centre[base + i] = -180.0 * folded(veff_own, i) - 6.0
            else:
                centre[base + my_core * half + i] = -180.0 * folded(veff_refs[0][k - 1], i) - 6.0
                centre[base + (1 - my_core) * half + i] = -180.0 * folded(veff_refs[1][k - 1], i) - 6.0
            return carry

        lax.fori_loop(0, slab if k == 0 else half, load_veff, 0)


def stash(place, orbs, veff_own, veffs):
    groups, vectors = len(orbs[0]), len(orbs)
    slab, rows, width = orbs[0][0].shape
    grid = (groups * slab, rows // SUB, SUB, width)
    operands = [place] + [piece for pieces in orbs for piece in pieces] + [veff_own] + veffs[0] + veffs[1]
    size = grid[0] * rows * width
    return pl.pallas_call(
        functools.partial(stash_kernel, groups, slab, vectors),
        out_shape=[jax.ShapeDtypeStruct(shape, jnp.float32) for shape in ((vectors,) + grid, grid)],
        in_specs=[SMEM] + [VMEM] * (len(operands) - 1),
        out_specs=[VMEM, VMEM],
        cost_estimate=pl.CostEstimate(flops=4 * size, bytes_accessed=8 * size * (vectors + 1), transcendentals=0),
        compiler_params=pltpu.CompilerParams(vmem_limit_bytes=8 * size * (vectors + 1) + (3 << 20)),
        name="stash",
    )(*operands)


def sweep_kernel(layout, *refs):
    groups, slab, cells, final_scale, vectors, prepared, accumulate, chunk, chunks = layout
    refs = list(refs)
    place_ref = refs.pop(0)
    weight_refs = [refs.pop(0) for _ in range(vectors)]
    matrix, centre = refs.pop(0), refs.pop(0)
    if prepared:
        orb_refs = [refs.pop(0) for _ in range(groups)]
        pot, scale_ref = refs.pop(0), refs.pop(0)
    else:
        orb_all = refs.pop(0)
        pot_refs = [refs.pop(0) for _ in range(groups)]
    before = refs.pop(0) if accumulate else None
    out = refs.pop(0)
    if not prepared:
        pot, scale_ref = refs.pop(0), refs.pop(0)
    first, second, third = refs[:3]
    total = groups * slab
    depth = first.shape[1] - 6
    my_dom, my_rest = place_ref[0], place_ref[1]

    if prepared:
        orb = refs[3]
    blank = jnp.zeros((3,) + first.shape[1:], jnp.float32)
    for buffer in (first, second, third):
        buffer[0:3] = blank
        buffer[total + 3 :] = blank

    if not prepared:
        pieces, piece = pot_refs[0].shape[:2]
        squares = jnp.zeros(pot.shape[1:], jnp.float32)
        for k in range(groups):
            base = (my_dom ^ k) * slab

            def load_pot(i, carry, k=k, base=base):
                for j in range(pieces):
                    value = folded(pot_refs[k], j, i)
                    x = base + (my_rest ^ j) * piece + i
                    pot[x] = value
                    put(first, x, value * orb_all[0, x])
                    carry = carry + value * value
                return carry

            squares = lax.fori_loop(0, piece, load_pot, squares)
        mean = jnp.sum(jnp.sum(jnp.sum(squares, axis=0), axis=0, keepdims=True), axis=1, keepdims=True) / cells
        scale_ref[...] = jnp.broadcast_to(lax.rsqrt(mean + norm_epsilon) * final_scale, scale_ref.shape)
    scale = scale_ref[...]
    orbital = my_dom * chunks + chunk
    for n in range(vectors):
        weight_ref = weight_refs[n]
        if prepared:
            for k in range(groups):
                base = (my_dom ^ k) * slab

                def load_slab(i, carry, k=k, base=base):
                    value = folded(orb_refs[k], i)
                    orb[base + i] = value
                    put(first, base + i, value * pot[base + i])
                    return carry

                lax.fori_loop(0, slab, load_slab, 0)
        elif n:

            def load_orb(x, carry, n=n):
                put(first, x, orb_all[n, x] * pot[x])
                return carry

            lax.fori_loop(0, total, load_orb, 0)

        run = functools.partial(stage, start=first, centre=centre, matrix=matrix, planes=PLANES, depth=depth)
        run(first, weight=weight_ref[orbital, 3], finish=lambda x, value: put(second, x, value))
        run(second, weight=weight_ref[orbital, 2], finish=lambda x, value: put(third, x, value))
        run(third, weight=weight_ref[orbital, 1], finish=lambda x, value: put(second, x, value))
        factor = scale * weight_ref[orbital, SWEEPS]

        def finish(x, value, n=n, factor=factor):
            value = value * (orb[x] if prepared else orb_all[n, x]) * factor
            if n == 0:
                out[x] = value + before[x] if accumulate else value
            else:
                out[x] = out[x] + value

        run(second, weight=weight_ref[orbital, 0], finish=finish)


def sweep(place, weights, matrix, centre, orbs, fields, before, cells, final_scale, chunk, chunks):
    prepared = isinstance(orbs, list)
    vectors = len(weights)
    total, depth, sub, width = grid = centre.shape
    rows = depth * sub
    groups = len(orbs) if prepared else len(fields)
    size = total * rows * width
    flat = list(orbs) if prepared else [orbs]
    operands = [place, *weights, matrix, centre] + flat + fields
    specs = [SMEM] + [VMEM] * (vectors + 2) + [VMEM] * len(flat) + [VMEM] * len(fields)
    if before is not None:
        operands.append(before)
        specs.append(VMEM)
    shapes = [grid] if prepared else [grid, grid, (sub, width)]
    scratch = [pltpu.VMEM((total + 6, depth + 6, sub, width), jnp.float32)] * 3
    if prepared:
        scratch.append(pltpu.VMEM(grid, jnp.float32))
    used = 12 * (total + 6) * (depth + 6) * sub * width + 4 * size * (6 if prepared else 4 + vectors)
    layout = (groups, total // groups, cells, final_scale, vectors, prepared, before is not None, chunk, chunks)
    return pl.pallas_call(
        functools.partial(sweep_kernel, layout),
        out_shape=[jax.ShapeDtypeStruct(shape, jnp.float32) for shape in shapes],
        in_specs=specs,
        out_specs=[VMEM] * len(shapes),
        scratch_shapes=scratch,
        cost_estimate=pl.CostEstimate(flops=200 * size * vectors, bytes_accessed=16 * size, transcendentals=0),
        compiler_params=pltpu.CompilerParams(vmem_limit_bytes=used + (3 << 20)),
    )(*operands)


def pick_kernel(rest, place_ref, owner_ref, *refs):
    out = refs[-1]
    my_rest, my_core = place_ref[1], place_ref[2]
    owner = owner_ref[my_core]
    wanted = 2 * ((owner >> 1) ^ my_rest) + ((owner & 1) ^ my_core)
    for index in range(2 * rest):

        @pl.when(wanted == index)
        def take(index=index):
            out[...] = refs[index][...]


def pick(place, owners, pieces):
    return pl.pallas_call(
        functools.partial(pick_kernel, len(pieces) // 2),
        out_shape=jax.ShapeDtypeStruct(pieces[0].shape, jnp.float32),
        in_specs=[SMEM, SMEM] + [VMEM] * len(pieces),
        out_specs=VMEM,
        compiler_params=pltpu.CompilerParams(vmem_limit_bytes=(2 << 20) + 4 * pieces[0].size * (len(pieces) + 1)),
        name="pick",
    )(place, owners, *pieces)


def join_kernel(*refs):
    for k, ref in enumerate(refs[:-1]):
        refs[-1][k] = ref[...]


def join(pieces):
    return pl.pallas_call(
        join_kernel,
        out_shape=jax.ShapeDtypeStruct((len(pieces),) + pieces[0].shape, jnp.float32),
        in_specs=[VMEM] * len(pieces),
        out_specs=VMEM,
        compiler_params=pltpu.CompilerParams(vmem_limit_bytes=(2 << 20) + 8 * len(pieces) * pieces[0].size),
        name="join",
    )(*pieces)


def deliver_kernel(rest, place_ref, owner_ref, *refs):
    out, tiles = refs[-2:]
    my_rest, my_core, my_rank = place_ref[1], place_ref[2], place_ref[3]
    keep = (owner_ref[my_core] == my_rank).astype(jnp.float32)
    take = (owner_ref[1 - my_core] == my_rank).astype(jnp.float32)
    phases, piece = refs[0].shape[:2]
    for k in range(rest):
        for phase in range(phases):
            value = refs[2 * k][phase] * keep + refs[2 * k + 1][phase] * take
            tiles[pl.ds((phase * rest + (my_rest ^ k)) * piece, piece)] = value
    slab = out.shape[1]
    depth = out.shape[2] // SUB
    for x in range(slab):
        for y in range(depth):
            out[0, x, pl.ds(y, SUB, stride=depth), :] = tiles[x * depth + y]


def deliver(place, owners, pieces, slab):
    rest = len(pieces) // 2
    phases, piece, sub, width = pieces[0].shape
    tiles = rest * phases * piece
    return pl.pallas_call(
        functools.partial(deliver_kernel, rest),
        out_shape=jax.ShapeDtypeStruct((1, slab, tiles // slab * sub, width), jnp.float32),
        in_specs=[SMEM, SMEM] + [VMEM] * len(pieces),
        out_specs=VMEM,
        scratch_shapes=[pltpu.VMEM((tiles, sub, width), jnp.float32)],
        compiler_params=pltpu.CompilerParams(vmem_limit_bytes=(2 << 20) + 16 * tiles * sub * width),
        name="deliver",
    )(place, owners, *pieces)


def per_device(orbitals, veff, trials, owners, levels, shift_index):
    groups, ranks = lax.axis_size("dom"), lax.axis_size("orb")
    rest = ranks // 2
    my_dom, my_rank = lax.axis_index("dom"), lax.axis_index("orb")
    my_rest, my_core = my_rank // 2, my_rank % 2
    local, slab = orbitals.shape[:2]
    cells = slab * groups * orbitals.shape[2] * orbitals.shape[3]
    chunks = local // groups
    final_scale = 4.0 / (local * ranks)

    def send(array, axis, size, flip):
        return lax.ppermute(array, axis, [(i, i ^ flip) for i in range(size)])

    def over_dom(pick):
        return {k: send(pick(k), "dom", groups, k) for k in reversed(range(1, groups))}

    def over_rest(pick):
        return {k: send(pick(k), "orb", ranks, 2 * k) for k in reversed(range(1, rest))}

    def over_core(array):
        return send(array, "orb", ranks, 1)

    def at(array, index):
        return lax.dynamic_index_in_dim(array, index, 0, keepdims=False)

    def chunk_of(orbitals, chunk):
        parts = over_dom(lambda k: at(orbitals, (my_dom ^ k) * chunks + chunk))
        parts[0] = at(orbitals, my_dom * chunks + chunk)
        return [parts[k] for k in range(groups)]

    half, piece = slab // 2, slab // rest
    place = jnp.stack([my_dom, my_rest, my_core, my_rank]).astype(jnp.int32)

    held = trials[0].reshape((rest, piece) + trials.shape[2:])
    arrived = over_rest(lambda k: at(held, my_rest ^ k))
    arrived[0] = at(held, my_rest)
    parts = [chunk_of(orbitals, 0)]
    crossed = {k: over_core(arrived[k]) for k in (0, *reversed(range(1, rest)))}
    mine = pick(place, owners, [array[k] for k in range(rest) for array in (arrived, crossed)])
    spread = over_rest(lambda k: mine)
    own_half = lax.dynamic_slice_in_dim(veff, my_core * half, half, 0)
    veff_mine = over_dom(lambda k: own_half)
    spread = join([mine] + [spread[k] for k in range(1, rest)])
    pots = over_dom(lambda k: spread)
    pots[0] = spread
    pots = [pots[k] for k in range(groups)]

    weights = monomials(levels, shift_index, orbitals.shape[-1])
    other_weights = over_core(weights)
    veff_mine = [veff_mine[k] for k in range(1, groups)]
    others = [[over_core(part) for part in parts[0]]]
    veff_other = [over_core(array) for array in veff_mine]
    later, _ = lax.optimization_barrier((orbitals, mine))
    parts += [chunk_of(later, chunk) for chunk in range(1, chunks)]

    matrix = lane_matrix(orbitals.shape[-1])
    orbs, centre = stash(place, [parts[0], others[0]], veff, [veff_mine, veff_other])
    response, *prepared = sweep(
        place, [weights, other_weights], matrix, centre, orbs, pots, None, cells, final_scale, 0, chunks
    )
    for chunk in range(1, chunks):
        others.append([over_core(part) for part in parts[chunk]])
        for weight, pieces in ((weights, parts), (other_weights, others)):
            response = sweep(
                place, [weight], matrix, centre, pieces[chunk], prepared, response, cells, final_scale, chunk, chunks
            )[0]

    tiles = slab * response.shape[1] // PHASES
    slabs = response.reshape((groups, PHASES, tiles) + response.shape[2:])
    arrived = [over_dom(lambda k: at(slabs, my_dom ^ k)[phase]) for phase in range(PHASES)]
    totals = []
    for phase in range(PHASES):
        summed = at(slabs, my_dom)[phase]
        if phase:
            arrived[phase][1], _ = lax.optimization_barrier((arrived[phase][1], pieces))
        for k in range(1, groups):
            summed = summed + arrived[phase][k]
        pieces = summed.reshape((rest, tiles // rest) + summed.shape[1:])
        others = over_rest(lambda k: at(pieces, my_rest ^ k))
        total = at(pieces, my_rest)
        for k in range(1, rest):
            total = total + others[k]
        totals.append(total)
    total = jnp.stack(totals)
    gathered = over_rest(lambda k: total)
    gathered[0] = total
    crossed = {k: over_core(gathered[k]) for k in (0, *reversed(range(1, rest)))}
    return deliver(place, owners, [array[k] for k in range(rest) for array in (gathered, crossed)], slab)


def solution(mesh):
    placed = (
        P("orb", "dom", None, None),
        P("dom", None, None),
        P("orb", "dom", None, None),
        P(),
        P(),
        P("orb"),
    )
    return jax.shard_map(
        per_device,
        mesh=mesh,
        in_specs=placed,
        out_specs=P("orb", "dom", None, None),
        check_vma=False,
    )
```
